128 devices in a mesh: aa: 16 (over y_hi, x, core), col: 8 (over z, y_lo).
Axes of the slice: x: 4, y: 4 (y_hi: 2, y_lo: 2; y = y_hi * 2 + y_lo), z: 4, core: 2. Of those that a mesh axis runs over, the one named last changes fastest.
Arguments:
- fit_ac: float32 [512, 512, 2048], P('aa', 'col'), may hold values from -0.125 to 0.125
- fit_bd: float32 [2048, 1024], P(('aa', 'col')), may hold values from -6 to 6
- amplitudes: float32 [2, 32, 512, 256], P(None, 'aa', 'col'), may hold values from -0.046875 to 0.046875
Outputs:
- residual: float32 [2, 16, 512, 256], P(None, 'col', 'aa')
The draws below stay inside these ranges and needn't reach their ends.
All inputs are finite; a program needn't handle non-finite values.
Results may differ from the reference program's by a relative error of at most 0.0003.
Values sent between devices are 32-bit elements; how exact they have to be, the bound alone decides.
No kernel may reach another device: no remote copies, remote signals or barrier semaphores. Data moves between devices by JAX's collectives and lax.ppermute only.
A program may use at most 128 MiB of HBM per device.

```python
import jax
import jax.numpy as jnp
from jax import lax

V = 512
NQ = 2048
KB = 2
NB = 16
ND = 32
P_SIZE = 256
N_AA = 16


def levels(own_key, extent, cuts, low, top_value):
    gain = 1.0
    for axis_at, parts in cuts:
        steps = jax.random.uniform(jax.random.fold_in(jax.random.fold_in(own_key, 6), axis_at), (parts,), jnp.float32, low / len(cuts), top_value / len(cuts))
        gain = gain * jnp.repeat(jnp.exp(steps), extent[axis_at] // parts).reshape((-1,) + (1,) * (len(extent) - 1 - axis_at))
    return gain


def normal_values(stream_key, extent, spread, most, cuts=(), held_as=jnp.bfloat16):
    factor_of = levels(stream_key, extent, cuts, -0.22, 0.18) if cuts else 1.0
    entries = jax.random.normal(stream_key, extent, jnp.float32) * spread * factor_of
    return jnp.minimum(jnp.maximum(entries, -most), most).astype(held_as)


def setup_inputs(seed: int = 0) -> dict:
    splits = jax.random.split(jax.random.key(seed), 4)
    return {
        "fit_ac": normal_values(splits[0], (V, V, NQ), NQ ** -0.5, 0.125, ((0, 16), (1, 8)), jnp.float32),
        "fit_bd": normal_values(splits[1], (NQ, KB * NB * ND), 1.0, 6.0, ((0, 128),), jnp.float32),
        "amplitudes": normal_values(splits[2], (KB, ND, V, P_SIZE), (V * ND) ** -0.5, 0.046875, ((1, 16), (2, 8)), jnp.float32),
    }


def reference(fit_ac, fit_bd, amplitudes):
    a_block = V // N_AA

    def one_block(index):
        start = (index * a_block).astype(jnp.int32)
        piece = lax.dynamic_slice_in_dim(fit_ac, start, a_block, 0)
        integrals = jnp.dot(piece.reshape(a_block * V, NQ), fit_bd, precision=lax.Precision.HIGHEST, preferred_element_type=jnp.float32)
        integrals = integrals.reshape(a_block, V, KB, NB, ND)
        return jnp.einsum("kdcp,ackbd->kbap", amplitudes, integrals, precision=lax.Precision.HIGHEST)

    pieces = lax.map(one_block, jnp.arange(V // a_block, dtype=jnp.int32))
    return pieces.transpose(1, 2, 0, 3, 4).reshape(KB, NB, V, P_SIZE)
```

```python
import functools

import jax
import jax.numpy as jnp
from jax import lax
from jax.experimental import pallas as pl
from jax.experimental.pallas import tpu as pltpu
from jax.sharding import PartitionSpec as P

BF16 = jnp.bfloat16
F32 = jnp.float32
ND = 32
LANES = 128
C_STEP = 8
CUTS = (0, 384, 768, 1024)
ORDERS = ("xyz", "yzx", "zxy")
T_ORDER = ("y2", "x1", "x2")
FIRST = (1, 3)
SECOND = (3, 1)


def device_at(x, y, z, core):
    return (((y // 2) * 4 + x) * 2 + core) * 8 + z * 2 + y % 2


def flipped(move):
    pairs = []
    for y in range(4):
        for x in range(4):
            for z in range(4):
                for core in range(2):
                    to = dict(x=x, y=y, z=z, core=core)
                    if move == "core":
                        to["core"] = 1 - core
                    elif move == "y2h":
                        to["y"] = y ^ 2
                    else:
                        to[move[0]] ^= (FIRST if move[1] == "1" else SECOND)[core]
                    pairs.append((device_at(x, y, z, core), device_at(**to)))
    return pairs


def swap(value, move):
    return lax.ppermute(value, ("aa", "col"), flipped(move))


def grown(value, move):
    return jnp.concatenate([value, swap(value, move)], axis=0)


def split(value):
    high = value.astype(BF16)
    return high, (value - high.astype(F32)).astype(BF16)


def dot(a, b):
    return jnp.dot(a, b, preferred_element_type=F32)


def dot3(a_high, a_low, b_high, b_low):
    return dot(a_high, b_high) + (dot(a_high, b_low) + dot(a_low, b_high))


def position():
    aa, col = lax.axis_index("aa"), lax.axis_index("col")
    y = (aa // 8) * 2 + col % 2
    return (aa // 2) % 4, y, col // 2, aa % 2


def chosen(core, pair):
    return jnp.where(core == 0, pair[0], pair[1])


def bit(j, at):
    return (j >> at) & 1


def fit_rows(j, half, order, core, x, y, z):
    first, second = chosen(core, FIRST), chosen(core, SECOND)
    moved = {"z": bit(j, 0) * first, "y": bit(j, 1) * first, "x": bit(j, 2) * first}
    for at, dim in enumerate(order):
        flip = half if at == 2 else bit(j, 3 + at)
        moved[dim] = moved[dim] ^ (flip * second)
    x, y, z = x ^ moved["x"], y ^ moved["y"], z ^ moved["z"]
    return (((y // 2) * 4 + x) * 2 + core) * 128 + z * 32 + (y % 2) * 16


def amplitude_d(j, half, core, x, y):
    first, second = chosen(core, FIRST), chosen(core, SECOND)
    high = (y // 2) ^ bit(j, 0)
    x = x ^ (bit(j, 1) * first) ^ (half * second)
    return ((high * 4 + x) * 2 + core) * 2


def kernel(*refs, n_fit, n_amp, nt, a_size, k_size, b_size):
    where_ref, a_ref = refs[0], refs[1]
    fits = refs[2 : 2 + n_fit]
    amps = refs[2 + n_fit : 2 + n_fit + n_amp]
    r_ref, fh, fl, ah, al, xh, xl, th, tl, vs, ts = refs[2 + n_fit + n_amp :]
    step = pl.program_id(0)
    x, y, z, core = (where_ref[i] for i in range(4))
    c_size, columns = C_STEP, fh.shape[1]
    lane_tiles = nt // LANES

    @pl.when(step == 0)
    def _():
        for at, ref in enumerate(fits):
            part, half, other = at // 4, (at // 2) % 2, at % 2
            cols = slice(CUTS[part], CUTS[part + 1])
            owner = core if other == 0 else 1 - core

            def place(j, carry):
                rows = fit_rows(j, half, ORDERS[part], owner, x, y, z)
                rows = pl.ds(pl.multiple_of(rows, 16), 16)
                high, low = split(ref[j])
                fh[rows, cols] = high
                fl[rows, cols] = low
                return carry

            lax.fori_loop(0, 32, place, 0, unroll=4)
        r_ref[...] = jnp.zeros_like(r_ref)

    for i in range(0, a_size, 4):
        high, low = split(a_ref[i : i + 4].reshape(4 * c_size, a_ref.shape[2]))
        ah[i * c_size : (i + 4) * c_size, :] = high
        al[i * c_size : (i + 4) * c_size, :] = low
    for k in range(k_size):
        for at, ref in enumerate(amps):
            half, owner = at // 2, (core if at % 2 == 0 else 1 - core)
            for j in range(4):
                d = amplitude_d(jnp.int32(j), half, owner, x, y)
                for dl in range(2):
                    rows = pl.ds(pl.multiple_of((d + dl) * c_size, c_size), c_size)
                    for lt in range(ts.shape[1]):
                        ts[k, lt, rows, :] = ref[j, k, dl, :, lt * LANES : (lt + 1) * LANES]
        for c in range(c_size):
            for lt in range(ts.shape[1]):
                high, low = split(ts[k, lt, pl.ds(c, ND, stride=c_size), :])
                rows, lanes = slice(c * ND, (c + 1) * ND), slice(lt * LANES, (lt + 1) * LANES)
                th[k, rows, lanes] = high
                tl[k, rows, lanes] = low

    lane = lax.broadcasted_iota(jnp.int32, (a_size, LANES), 1)
    front, even = lane < 64, (lane // 32) % 2 == 0
    for n in range(columns // nt):
        cols = slice(n * nt, (n + 1) * nt)
        value = dot3(ah[...], al[...], fh[:, cols], fl[:, cols])
        for lt in range(lane_tiles):
            vs[n * lane_tiles + lt] = value[:, lt * LANES : (lt + 1) * LANES]
        for lt in range(lane_tiles):
            tile = n * lane_tiles + lt
            for cq in range(c_size // 4):
                q = [vs[tile, pl.ds(cq * 4 + j, a_size, stride=c_size), :] for j in range(4)]
                s = [
                    jnp.where(front, q[0], pltpu.roll(q[2], 64, 1)),
                    jnp.where(front, q[1], pltpu.roll(q[3], 64, 1)),
                    jnp.where(front, pltpu.roll(q[0], 64, 1), q[2]),
                    jnp.where(front, pltpu.roll(q[1], 64, 1), q[3]),
                ]
                w = [
                    jnp.where(even, s[0], pltpu.roll(s[1], 32, 1)),
                    jnp.where(even, pltpu.roll(s[0], 96, 1), s[1]),
                    jnp.where(even, s[2], pltpu.roll(s[3], 32, 1)),
                    jnp.where(even, pltpu.roll(s[2], 96, 1), s[3]),
                ]
                for b in range(4):
                    high, low = split(w[b])
                    row = (tile * 4 + b) * a_size
                    xh[row : row + a_size, cq * LANES : (cq + 1) * LANES] = high
                    xl[row : row + a_size, cq * LANES : (cq + 1) * LANES] = low
    for k in range(k_size):
        rows = slice(k * b_size * a_size, (k + 1) * b_size * a_size)
        value = dot3(xh[rows, :], xl[rows, :], th[k], tl[k])
        r_ref[:, k] += value.reshape(b_size, a_size, value.shape[1])


def contracted(where, fit_ac, fits, amps, nt=512):
    a_size, c_local, q_size = fit_ac.shape
    k_size, pairs = amps[0].shape[1], amps[0].shape[4]
    columns = CUTS[-1]
    b_size = columns // (k_size * ND)
    rows = a_size * C_STEP
    whole = lambda value: pl.BlockSpec(
        value.shape, lambda i, w: (0,) * value.ndim, pipeline_mode=pl.Buffered(1)
    )
    grid_spec = pltpu.PrefetchScalarGridSpec(
        num_scalar_prefetch=1,
        grid=(c_local // C_STEP,),
        in_specs=[pl.BlockSpec((a_size, C_STEP, q_size), lambda i, w: (0, i, 0))]
        + [whole(value) for value in fits]
        + [
            pl.BlockSpec((4, k_size, 2, C_STEP, pairs), lambda i, w: (0, 0, 0, i, 0))
            for _ in amps
        ],
        out_specs=pl.BlockSpec((b_size, k_size, a_size, pairs), lambda i, w: (0, 0, 0, 0)),
        scratch_shapes=[
            pltpu.VMEM((q_size, columns), BF16),
            pltpu.VMEM((q_size, columns), BF16),
            pltpu.VMEM((rows, q_size), BF16),
            pltpu.VMEM((rows, q_size), BF16),
            pltpu.VMEM((k_size * b_size * a_size, C_STEP * ND), BF16),
            pltpu.VMEM((k_size * b_size * a_size, C_STEP * ND), BF16),
            pltpu.VMEM((k_size, C_STEP * ND, pairs), BF16),
            pltpu.VMEM((k_size, C_STEP * ND, pairs), BF16),
            pltpu.VMEM((columns // LANES, rows, LANES), F32),
            pltpu.VMEM((k_size, pairs // LANES, ND * C_STEP, LANES), F32),
        ],
    )
    return pl.pallas_call(
        functools.partial(
            kernel, n_fit=len(fits), n_amp=len(amps), nt=nt, a_size=a_size, k_size=k_size, b_size=b_size
        ),
        grid_spec=grid_spec,
        out_shape=jax.ShapeDtypeStruct((b_size, k_size, a_size, pairs), F32),
        compiler_params=pltpu.CompilerParams(vmem_limit_bytes=58 << 20),
    )(where, fit_ac, *fits, *amps)


def gathered_fit(fit_bd):
    value = fit_bd[None]
    for move in ("z1", "y1", "x1"):
        value = grown(value, move)
    parts = [value[:, :, CUTS[i] : CUTS[i + 1]] for i in range(3)]
    for at in range(2):
        parts = [grown(part, order[at] + "2") for part, order in zip(parts, ORDERS)]
    arrived = [swap(part, order[2] + "2") for part, order in zip(parts, ORDERS)]
    near = [swap(part, "core") for part in parts]
    far = [swap(part, "core") for part in arrived]
    return [v for four in zip(parts, near, arrived, far) for v in four]


def gathered_amplitudes(amplitudes):
    value = amplitudes[None]
    value = grown(value, "y2h")
    value = grown(value, "x1")
    arrived = swap(value, "x2")
    return [value, swap(value, "core"), arrived, swap(arrived, "core")]


def shards(fit_ac, fit_bd, amplitudes):
    x, y, z, core = position()
    where = jnp.stack([x, y, z, core]).astype(jnp.int32)
    fits = gathered_fit(fit_bd)
    amps = gathered_amplitudes(amplitudes)
    partial = contracted(where, fit_ac, fits, amps)
    b_size, k_size, a_size, pairs = partial.shape
    peers = lax.axis_size("col")
    pieces = partial.reshape(peers, b_size // peers, k_size, a_size, pairs)
    pieces = lax.all_to_all(pieces, "col", 0, 0, tiled=True)
    return jnp.sum(pieces, axis=0).transpose(1, 0, 2, 3)


def solution(mesh):
    placed = (P("aa", "col", None), P(("aa", "col"), None), P(None, "aa", "col", None))
    return jax.shard_map(
        shards, mesh=mesh, in_specs=placed, out_specs=P(None, "col", "aa", None), check_vma=False
    )
```

```python
import functools

import jax
import jax.numpy as jnp
from jax import lax
from jax.experimental import pallas as pl
from jax.experimental.pallas import tpu as pltpu
from jax.sharding import PartitionSpec as P

BF16 = jnp.bfloat16
F32 = jnp.float32
ND = 32
LANES = 128
C_STEP = 8
N_STEP = 256
F8 = jnp.float8_e5m2
F_HIGH, F_LOW = 2.0**12, 2.0**21
A_HIGH, A_LOW = 2.0**17, 2.0**26
UNSCALE = 2.0**-38
CUTS = (0, 384, 768, 1024)
ORDERS = ("xyz", "yzx", "zxy")
T_ORDER = ("y2", "x1", "x2")
FIRST = (1, 3)
SECOND = (3, 1)


def device_at(x, y, z, core):
    return (((y // 2) * 4 + x) * 2 + core) * 8 + z * 2 + y % 2


def flipped(move):
    pairs = []
    for y in range(4):
        for x in range(4):
            for z in range(4):
                for core in range(2):
                    to = dict(x=x, y=y, z=z, core=core)
                    if move == "core":
                        to["core"] = 1 - core
                    elif move == "y2h":
                        to["y"] = y ^ 2
                    else:
                        to[move[0]] ^= (FIRST if move[1] == "1" else SECOND)[core]
                    pairs.append((device_at(x, y, z, core), device_at(**to)))
    return pairs


def swap(value, move):
    return lax.ppermute(value, ("aa", "col"), flipped(move))


def grown(value, move):
    return jnp.concatenate([value, swap(value, move)], axis=0)


def split(value):
    high = value.astype(BF16)
    return high, (value - high.astype(F32)).astype(BF16)


def dot(a, b):
    return jnp.dot(a, b, preferred_element_type=F32)


def dot3(a_high, a_low, b_high, b_low):
    return dot(a_high, b_high) + (dot(a_high, b_low) + dot(a_low, b_high))


def position():
    aa, col = lax.axis_index("aa"), lax.axis_index("col")
    y = (aa // 8) * 2 + col % 2
    return (aa // 2) % 4, y, col // 2, aa % 2


def chosen(core, pair):
    return jnp.where(core == 0, pair[0], pair[1])


def bit(j, at):
    return (j >> at) & 1


def amplitude_d(j, half, core, x, y):
    first, second = chosen(core, FIRST), chosen(core, SECOND)
    high = (y // 2) ^ bit(j, 0)
    x = x ^ (bit(j, 1) * first) ^ (half * second)
    return ((high * 4 + x) * 2 + core) * 2


def kernel(*refs, n_fit, n_amp, a_size, k_size, b_size):
    where_ref, a_ref = refs[0], refs[1]
    fits = refs[2 : 2 + n_fit]
    amps = refs[2 + n_fit : 2 + n_fit + n_amp]
    r_ref, fh, fl, f8, ah, a8, xh, xl, th, tl, vs, ts = refs[2 + n_fit + n_amp :]
    step = pl.program_id(0)
    last = pl.num_programs(0) - 1
    x, y, z, core = (where_ref[i] for i in range(4))
    c_size, (q_size, columns) = C_STEP, fh.shape
    pairs = th.shape[2]

    @pl.when(step == 0)
    def _():
        for other in range(2):
            owner = core if other == 0 else 1 - core
            first, second = chosen(owner, FIRST), chosen(owner, SECOND)
            moves = [[0, second], [first, first ^ second]]
            at_x = [[(x ^ m) * 256 + owner * 128 for m in row] for row in moves]
            at_y = [[((y ^ m) // 2) * 1024 + ((y ^ m) % 2) * 16 for m in row] for row in moves]
            at_z = [[(z ^ m) * 32 for m in row] for row in moves]
            for at, ref in enumerate(fits):
                part, half = at // 4, (at // 2) % 2
                if at % 2 != other:
                    continue
                cols = slice(CUTS[part], CUTS[part + 1])
                for j in range(32):
                    flips = dict(zip(ORDERS[part], (bit(j, 3), bit(j, 4), half)))
                    rows = at_x[bit(j, 2)][flips["x"]] + at_y[bit(j, 1)][flips["y"]] + at_z[bit(j, 0)][flips["z"]]
                    place = pl.ds(pl.multiple_of(rows, 16), 16)
                    high, low = split(ref[j])
                    fh[place, cols] = high
                    fl[place, cols] = low

        def narrow(i, carry):
            rows = pl.ds(pl.multiple_of(i * 32, 32), 32)
            f8[rows, :] = (fl[rows, :].astype(F32) * F_LOW).astype(F8)
            f8[pl.ds(pl.multiple_of(q_size + i * 32, 32), 32), :] = (fh[rows, :].astype(F32) * F_HIGH).astype(F8)
            return carry

        lax.fori_loop(0, q_size // 32, narrow, 0, unroll=2)
        r_ref[...] = jnp.zeros_like(r_ref)

    lane = lax.broadcasted_iota(jnp.int32, (a_size, LANES), 1)
    front, even = lane < 64, (lane // 32) % 2 == 0

    def fit_ready():
        for i in range(0, a_size, 4):
            rows = slice(i * c_size, (i + 4) * c_size)
            value = a_ref[i : i + 4].reshape(4 * c_size, q_size)
            high = value.astype(BF16)
            ah[rows, :] = high
            a8[rows, :q_size] = (value * A_HIGH).astype(F8)
            a8[rows, q_size:] = ((value - high.astype(F32)) * A_LOW).astype(F8)

    def first_parts():
        values = [None] * (columns // N_STEP)

        def one(n):
            cols = slice(n * N_STEP, (n + 1) * N_STEP)
            values[n] = dot(ah[...], fh[:, cols])

        def rest(n):
            cols = slice(n * N_STEP, (n + 1) * N_STEP)
            values[n] = values[n] + dot(a8[...], f8[:, cols]) * UNSCALE

        return values, [functools.partial(f, n) for n in range(len(values)) for f in (one, rest)]

    def store(values):
        for n, value in enumerate(values):
            for lt in range(N_STEP // LANES):
                vs[n * (N_STEP // LANES) + lt] = value[:, lt * LANES : (lt + 1) * LANES]

    def amplitudes_ready(k):
        for at, ref in enumerate(amps):
            half, owner = at // 2, (core if at % 2 == 0 else 1 - core)
            for j in range(4):
                d = amplitude_d(jnp.int32(j), half, owner, x, y)
                for dl in range(2):
                    rows = pl.ds(pl.multiple_of((d + dl) * c_size, c_size), c_size)
                    for lt in range(ts.shape[1]):
                        ts[k, lt, rows, :] = ref[j, k, dl, :, lt * LANES : (lt + 1) * LANES]
        for c in range(c_size):
            for lt in range(ts.shape[1]):
                high, low = split(ts[k, lt, pl.ds(c, ND, stride=c_size), :])
                rows, lanes = slice(c * ND, (c + 1) * ND), slice(lt * LANES, (lt + 1) * LANES)
                th[k, rows, lanes] = high
                tl[k, rows, lanes] = low

    def turned(tile, cq):
        q = [vs[tile, pl.ds(cq * 4 + j, a_size, stride=c_size), :] for j in range(4)]
        s = [
            jnp.where(front, q[0], pltpu.roll(q[2], 64, 1)),
            jnp.where(front, q[1], pltpu.roll(q[3], 64, 1)),
            jnp.where(front, pltpu.roll(q[0], 64, 1), q[2]),
            jnp.where(front, pltpu.roll(q[1], 64, 1), q[3]),
        ]
        w = [
            jnp.where(even, s[0], pltpu.roll(s[1], 32, 1)),
            jnp.where(even, pltpu.roll(s[0], 96, 1), s[1]),
            jnp.where(even, s[2], pltpu.roll(s[3], 32, 1)),
            jnp.where(even, pltpu.roll(s[2], 96, 1), s[3]),
        ]
        for b in range(4):
            high, low = split(w[b])
            row = (tile * 4 + b) * a_size
            xh[row : row + a_size, cq * LANES : (cq + 1) * LANES] = high
            xl[row : row + a_size, cq * LANES : (cq + 1) * LANES] = low

    def second_parts():
        return [functools.partial(amplitudes_ready, k) for k in range(k_size)] + [
            functools.partial(turned, tile, cq)
            for tile in range(columns // LANES)
            for cq in range(c_size // 4)
        ]

    def second_product():
        for k in range(k_size):
            rows = slice(k * b_size * a_size, (k + 1) * b_size * a_size)
            value = dot3(xh[rows, :], xl[rows, :], th[k], tl[k])
            r_ref[:, k] += value.reshape(b_size, a_size, pairs)

    @pl.when(step == 0)
    def _():
        fit_ready()
        values, parts = first_parts()
        for part in parts:
            part()
        store(values)

    @pl.when((step > 0) & (step < last))
    def _():
        fit_ready()
        values, dots = first_parts()
        moves = second_parts()
        for at, part in enumerate(dots):
            part()
            for move in moves[at * len(moves) // len(dots) : (at + 1) * len(moves) // len(dots)]:
                move()
        second_product()
        store(values)

    @pl.when(step == last)
    def _():
        for move in second_parts():
            move()
        second_product()


def contracted(where, fit_ac, fits, amps):
    a_size, c_local, q_size = fit_ac.shape
    k_size, pairs = amps[0].shape[1], amps[0].shape[4]
    columns = CUTS[-1]
    b_size = columns // (k_size * ND)
    rows = a_size * C_STEP
    steps = c_local // C_STEP
    whole = lambda value: pl.BlockSpec(
        value.shape, lambda i, w: (0,) * value.ndim, pipeline_mode=pl.Buffered(1)
    )
    grid_spec = pltpu.PrefetchScalarGridSpec(
        num_scalar_prefetch=1,
        grid=(steps + 1,),
        in_specs=[pl.BlockSpec((a_size, C_STEP, q_size), lambda i, w: (0, jnp.minimum(i, steps - 1), 0))]
        + [whole(value) for value in fits]
        + [
            pl.BlockSpec(
                (4, k_size, 2, C_STEP, pairs), lambda i, w: (0, 0, 0, jnp.maximum(i - 1, 0), 0)
            )
            for _ in amps
        ],
        out_specs=pl.BlockSpec((b_size, k_size, a_size, pairs), lambda i, w: (0, 0, 0, 0)),
        scratch_shapes=[
            pltpu.VMEM((q_size, columns), BF16),
            pltpu.VMEM((q_size, columns), BF16),
            pltpu.VMEM((2 * q_size, columns), F8),
            pltpu.VMEM((rows, q_size), BF16),
            pltpu.VMEM((rows, 2 * q_size), F8),
            pltpu.VMEM((k_size * b_size * a_size, C_STEP * ND), BF16),
            pltpu.VMEM((k_size * b_size * a_size, C_STEP * ND), BF16),
            pltpu.VMEM((k_size, C_STEP * ND, pairs), BF16),
            pltpu.VMEM((k_size, C_STEP * ND, pairs), BF16),
            pltpu.VMEM((columns // LANES, rows, LANES), F32),
            pltpu.VMEM((k_size, pairs // LANES, ND * C_STEP, LANES), F32),
        ],
    )
    return pl.pallas_call(
        functools.partial(
            kernel, n_fit=len(fits), n_amp=len(amps), a_size=a_size, k_size=k_size, b_size=b_size
        ),
        grid_spec=grid_spec,
        out_shape=jax.ShapeDtypeStruct((b_size, k_size, a_size, pairs), F32),
        compiler_params=pltpu.CompilerParams(vmem_limit_bytes=58 << 20),
    )(where, fit_ac, *fits, *amps)


def gathered_fit(fit_bd):
    value = fit_bd[None]
    for move in ("z1", "y1", "x1"):
        value = grown(value, move)
    parts = [value[:, :, CUTS[i] : CUTS[i + 1]] for i in range(3)]
    for at in range(2):
        parts = [grown(part, order[at] + "2") for part, order in zip(parts, ORDERS)]
    arrived = [swap(part, order[2] + "2") for part, order in zip(parts, ORDERS)]
    near = [swap(part, "core") for part in parts]
    far = [swap(part, "core") for part in arrived]
    return [v for four in zip(parts, near, arrived, far) for v in four]


def gathered_amplitudes(amplitudes):
    value = amplitudes[None]
    value = grown(value, "y2h")
    value = grown(value, "x1")
    arrived = swap(value, "x2")
    return [value, swap(value, "core"), arrived, swap(arrived, "core")]


def shards(fit_ac, fit_bd, amplitudes):
    x, y, z, core = position()
    where = jnp.stack([x, y, z, core]).astype(jnp.int32)
    fits = gathered_fit(fit_bd)
    amps = gathered_amplitudes(amplitudes)
    partial = contracted(where, fit_ac, fits, amps)
    b_size, k_size, a_size, pairs = partial.shape
    peers = lax.axis_size("col")
    pieces = partial.reshape(peers, b_size // peers, k_size, a_size, pairs)
    pieces = lax.all_to_all(pieces, "col", 0, 0, tiled=True)
    return jnp.sum(pieces, axis=0).transpose(1, 0, 2, 3)


def solution(mesh):
    placed = (P("aa", "col", None), P(("aa", "col"), None), P(None, "aa", "col", None))
    return jax.shard_map(
        shards, mesh=mesh, in_specs=placed, out_specs=P(None, "col", "aa", None), check_vma=False
    )
```

```python
import functools

import jax
import jax.numpy as jnp
from jax import lax
from jax.experimental import pallas as pl
from jax.experimental.pallas import tpu as pltpu
from jax.sharding import PartitionSpec as P

BF16 = jnp.bfloat16
F32 = jnp.float32
ND = 32
LANES = 128
C_STEP = 8
N_STEP = 256
F8 = jnp.float8_e5m2
F_HIGH, F_LOW = 2.0**12, 2.0**21
A_HIGH, A_LOW = 2.0**17, 2.0**26
UNSCALE = 2.0**-38
CUTS = (0, 384, 768, 1024)
ORDERS = ("xyz", "yzx", "zxy")
T_ORDER = ("y2", "x1", "x2")
FIRST = (1, 3)
SECOND = (3, 1)


def device_at(x, y, z, core):
    return (((y // 2) * 4 + x) * 2 + core) * 8 + z * 2 + y % 2


def flipped(move):
    pairs = []
    for y in range(4):
        for x in range(4):
            for z in range(4):
                for core in range(2):
                    to = dict(x=x, y=y, z=z, core=core)
                    if move == "core":
                        to["core"] = 1 - core
                    elif move == "y2h":
                        to["y"] = y ^ 2
                    else:
                        to[move[0]] ^= (FIRST if move[1] == "1" else SECOND)[core]
                    pairs.append((device_at(x, y, z, core), device_at(**to)))
    return pairs


def swap(value, move):
    return lax.ppermute(value, ("aa", "col"), flipped(move))


def grown(value, move):
    return jnp.concatenate([value, swap(value, move)], axis=0)


def split(value):
    high = value.astype(BF16)
    return high, (value - high.astype(F32)).astype(BF16)


def dot(a, b):
    return jnp.dot(a, b, preferred_element_type=F32)


def dot3(a_high, a_low, b_high, b_low):
    return dot(a_high, b_high) + (dot(a_high, b_low) + dot(a_low, b_high))


def position():
    aa, col = lax.axis_index("aa"), lax.axis_index("col")
    y = (aa // 8) * 2 + col % 2
    return (aa // 2) % 4, y, col // 2, aa % 2


def chosen(core, pair):
    return jnp.where(core == 0, pair[0], pair[1])


def bit(j, at):
    return (j >> at) & 1


def amplitude_d(j, half, core, x, y):
    first, second = chosen(core, FIRST), chosen(core, SECOND)
    high = (y // 2) ^ bit(j, 0)
    x = x ^ (bit(j, 1) * first) ^ (half * second)
    return ((high * 4 + x) * 2 + core) * 2


def kernel(*refs, n_fit, n_amp, a_size, k_size, b_size):
    where_ref, a_ref = refs[0], refs[1]
    fits = refs[2 : 2 + n_fit]
    amps = refs[2 + n_fit : 2 + n_fit + n_amp]
    r_ref, fh, fl, f8, ah, a8, xh, xl, th, tl, vs, ts = refs[2 + n_fit + n_amp :]
    step = pl.program_id(0)
    last = pl.num_programs(0) - 1
    x, y, z, core = (where_ref[i] for i in range(4))
    c_size, (q_size, columns) = C_STEP, fh.shape
    pairs = th.shape[2]

    @pl.when(step == 0)
    def _():
        for other in range(2):
            owner = core if other == 0 else 1 - core
            first, second = chosen(owner, FIRST), chosen(owner, SECOND)

            def reached(at):
                froms = [at, at ^ second]
                lower = [jnp.minimum(v, v ^ first) for v in froms]
                return [lower, [v ^ first for v in lower]]

            at_x = [[v * 256 + owner * 128 for v in row] for row in reached(x)]
            at_y = [[(v // 2) * 1024 + (v % 2) * 16 for v in row] for row in reached(y)]
            at_z = [[v * 32 for v in row] for row in reached(z)]
            for at, ref in enumerate(fits):
                part, half = at // 4, (at // 2) % 2
                if at % 2 != other:
                    continue
                cols = slice(CUTS[part], CUTS[part + 1])
                for j in range(32):
                    flips = dict(zip(ORDERS[part], (bit(j, 3), bit(j, 4), half)))
                    rows = at_x[bit(j, 2)][flips["x"]] + at_y[bit(j, 1)][flips["y"]] + at_z[bit(j, 0)][flips["z"]]
                    place = pl.ds(pl.multiple_of(rows, 16), 16)
                    high, low = split(ref[j])
                    fh[place, cols] = high
                    fl[place, cols] = low

        def narrow(i, carry):
            rows = pl.ds(pl.multiple_of(i * 32, 32), 32)
            f8[rows, :] = (fl[rows, :].astype(F32) * F_LOW).astype(F8)
            f8[pl.ds(pl.multiple_of(q_size + i * 32, 32), 32), :] = (fh[rows, :].astype(F32) * F_HIGH).astype(F8)
            return carry

        lax.fori_loop(0, q_size // 32, narrow, 0, unroll=2)
        r_ref[...] = jnp.zeros_like(r_ref)

    lane = lax.broadcasted_iota(jnp.int32, (a_size, LANES), 1)
    front, even = lane < 64, (lane // 32) % 2 == 0

    def fit_ready():
        for i in range(0, a_size, 4):
            rows = slice(i * c_size, (i + 4) * c_size)
            value = a_ref[i : i + 4].reshape(4 * c_size, q_size)
            high = value.astype(BF16)
            ah[rows, :] = high
            a8[rows, :q_size] = (value * A_HIGH).astype(F8)
            a8[rows, q_size:] = ((value - high.astype(F32)) * A_LOW).astype(F8)

    def first_parts():
        values = [None] * (columns // N_STEP)

        def one(n):
            cols = slice(n * N_STEP, (n + 1) * N_STEP)
            values[n] = dot(ah[...], fh[:, cols])

        def rest(n):
            cols = slice(n * N_STEP, (n + 1) * N_STEP)
            values[n] = values[n] + dot(a8[...], f8[:, cols]) * UNSCALE

        return values, [functools.partial(f, n) for n in range(len(values)) for f in (one, rest)]

    def store(values):
        for n, value in enumerate(values):
            for lt in range(N_STEP // LANES):
                vs[n * (N_STEP // LANES) + lt] = value[:, lt * LANES : (lt + 1) * LANES]

    def amplitudes_ready(k):
        for at, ref in enumerate(amps):
            half, owner = at // 2, (core if at % 2 == 0 else 1 - core)
            for j in range(4):
                d = amplitude_d(jnp.int32(j), half, owner, x, y)
                for dl in range(2):
                    rows = pl.ds(pl.multiple_of((d + dl) * c_size, c_size), c_size)
                    for lt in range(ts.shape[1]):
                        ts[k, lt, rows, :] = ref[j, k, dl, :, lt * LANES : (lt + 1) * LANES]
        for c in range(c_size):
            for lt in range(ts.shape[1]):
                high, low = split(ts[k, lt, pl.ds(c, ND, stride=c_size), :])
                rows, lanes = slice(c * ND, (c + 1) * ND), slice(lt * LANES, (lt + 1) * LANES)
                th[k, rows, lanes] = high
                tl[k, rows, lanes] = low

    def turned(tile, cq):
        q = [vs[tile, pl.ds(cq * 4 + j, a_size, stride=c_size), :] for j in range(4)]
        s = [
            jnp.where(front, q[0], pltpu.roll(q[2], 64, 1)),
            jnp.where(front, q[1], pltpu.roll(q[3], 64, 1)),
            jnp.where(front, pltpu.roll(q[0], 64, 1), q[2]),
            jnp.where(front, pltpu.roll(q[1], 64, 1), q[3]),
        ]
        w = [
            jnp.where(even, s[0], pltpu.roll(s[1], 32, 1)),
            jnp.where(even, pltpu.roll(s[0], 96, 1), s[1]),
            jnp.where(even, s[2], pltpu.roll(s[3], 32, 1)),
            jnp.where(even, pltpu.roll(s[2], 96, 1), s[3]),
        ]
        for b in range(4):
            high, low = split(w[b])
            row = (tile * 4 + b) * a_size
            xh[row : row + a_size, cq * LANES : (cq + 1) * LANES] = high
            xl[row : row + a_size, cq * LANES : (cq + 1) * LANES] = low

    def second_parts():
        return [functools.partial(amplitudes_ready, k) for k in range(k_size)] + [
            functools.partial(turned, tile, cq)
            for tile in range(columns // LANES)
            for cq in range(c_size // 4)
        ]

    def second_product():
        for k in range(k_size):
            rows = slice(k * b_size * a_size, (k + 1) * b_size * a_size)
            value = dot3(xh[rows, :], xl[rows, :], th[k], tl[k])
            r_ref[:, k] += value.reshape(b_size, a_size, pairs)

    @pl.when(step == 0)
    def _():
        fit_ready()
        values, parts = first_parts()
        for part in parts:
            part()
        store(values)

    @pl.when((step > 0) & (step < last))
    def _():
        fit_ready()
        values, dots = first_parts()
        moves = second_parts()
        for at, part in enumerate(dots):
            part()
            for move in moves[at * len(moves) // len(dots) : (at + 1) * len(moves) // len(dots)]:
                move()
        second_product()
        store(values)

    @pl.when(step == last)
    def _():
        for move in second_parts():
            move()
        second_product()


def contracted(where, fit_ac, fits, amps):
    a_size, c_local, q_size = fit_ac.shape
    k_size, pairs = amps[0].shape[1], amps[0].shape[4]
    columns = CUTS[-1]
    b_size = columns // (k_size * ND)
    rows = a_size * C_STEP
    steps = c_local // C_STEP
    whole = lambda value: pl.BlockSpec(
        value.shape, lambda i, w: (0,) * value.ndim, pipeline_mode=pl.Buffered(1)
    )
    grid_spec = pltpu.PrefetchScalarGridSpec(
        num_scalar_prefetch=1,
        grid=(steps + 1,),
        in_specs=[pl.BlockSpec((a_size, C_STEP, q_size), lambda i, w: (0, jnp.minimum(i, steps - 1), 0))]
        + [whole(value) for value in fits]
        + [
            pl.BlockSpec(
                (4, k_size, 2, C_STEP, pairs), lambda i, w: (0, 0, 0, jnp.maximum(i - 1, 0), 0)
            )
            for _ in amps
        ],
        out_specs=pl.BlockSpec((b_size, k_size, a_size, pairs), lambda i, w: (0, 0, 0, 0)),
        scratch_shapes=[
            pltpu.VMEM((q_size, columns), BF16),
            pltpu.VMEM((q_size, columns), BF16),
            pltpu.VMEM((2 * q_size, columns), F8),
            pltpu.VMEM((rows, q_size), BF16),
            pltpu.VMEM((rows, 2 * q_size), F8),
            pltpu.VMEM((k_size * b_size * a_size, C_STEP * ND), BF16),
            pltpu.VMEM((k_size * b_size * a_size, C_STEP * ND), BF16),
            pltpu.VMEM((k_size, C_STEP * ND, pairs), BF16),
            pltpu.VMEM((k_size, C_STEP * ND, pairs), BF16),
            pltpu.VMEM((columns // LANES, rows, LANES), F32),
            pltpu.VMEM((k_size, pairs // LANES, ND * C_STEP, LANES), F32),
        ],
    )
    return pl.pallas_call(
        functools.partial(
            kernel, n_fit=len(fits), n_amp=len(amps), a_size=a_size, k_size=k_size, b_size=b_size
        ),
        grid_spec=grid_spec,
        out_shape=jax.ShapeDtypeStruct((b_size, k_size, a_size, pairs), F32),
        compiler_params=pltpu.CompilerParams(vmem_limit_bytes=58 << 20),
    )(where, fit_ac, *fits, *amps)


def sent_to_all(value, groups):
    copies = jnp.broadcast_to(value, (len(groups[0]), *value.shape))
    return lax.all_to_all(copies, ("aa", "col"), 0, 0, tiled=True, axis_index_groups=groups)


def cubes():
    pairs = [[(0, 1), (2, 3)], [(0, 3), (1, 2)]]
    return [
        [device_at(x, y, z, core) for x in xs for y in ys for z in zs]
        for core in range(2)
        for xs in pairs[core]
        for ys in pairs[core]
        for zs in pairs[core]
    ]


def gathered_fit(fit_bd):
    value = sent_to_all(fit_bd, cubes())
    parts = [value[:, :, CUTS[i] : CUTS[i + 1]] for i in range(3)]
    for at in range(2):
        parts = [grown(part, order[at] + "2") for part, order in zip(parts, ORDERS)]
    arrived = [swap(part, order[2] + "2") for part, order in zip(parts, ORDERS)]
    near = [swap(part, "core") for part in parts]
    far = [swap(part, "core") for part in arrived]
    return [v for four in zip(parts, near, arrived, far) for v in four]


def gathered_amplitudes(amplitudes):
    value = amplitudes[None]
    value = grown(value, "y2h")
    value = grown(value, "x1")
    arrived = swap(value, "x2")
    return [value, swap(value, "core"), arrived, swap(arrived, "core")]


def shards(fit_ac, fit_bd, amplitudes):
    x, y, z, core = position()
    where = jnp.stack([x, y, z, core]).astype(jnp.int32)
    fits = gathered_fit(fit_bd)
    amps = gathered_amplitudes(amplitudes)
    partial = contracted(where, fit_ac, fits, amps)
    b_size, k_size, a_size, pairs = partial.shape
    peers = lax.axis_size("col")
    pieces = partial.reshape(peers, b_size // peers, k_size, a_size, pairs)
    pieces = lax.all_to_all(pieces, "col", 0, 0, tiled=True)
    return jnp.sum(pieces, axis=0).transpose(1, 0, 2, 3)


def solution(mesh):
    placed = (P("aa", "col", None), P(("aa", "col"), None), P(None, "aa", "col", None))
    return jax.shard_map(
        shards, mesh=mesh, in_specs=placed, out_specs=P(None, "col", "aa", None), check_vma=False
    )
```

```python
import functools

import jax
import jax.numpy as jnp
from jax import lax
from jax.experimental import pallas as pl
from jax.experimental.pallas import tpu as pltpu
from jax.sharding import PartitionSpec as P

BF16 = jnp.bfloat16
F32 = jnp.float32
ND = 32
LANES = 128
C_STEP = 8
N_STEP = 256
F8 = jnp.float8_e5m2
F_HIGH, F_LOW = 2.0**12, 2.0**21
A_HIGH, A_LOW = 2.0**17, 2.0**26
UNSCALE = 2.0**-38
CUTS = (0, 512, 1024)
ORDERS = ("xyz", "xzy")
T_ORDER = ("y2", "x1", "x2")
FIRST = (1, 3)
SECOND = (3, 1)


def device_at(x, y, z, core):
    return (((y // 2) * 4 + x) * 2 + core) * 8 + z * 2 + y % 2


def flipped(move):
    pairs = []
    for y in range(4):
        for x in range(4):
            for z in range(4):
                for core in range(2):
                    to = dict(x=x, y=y, z=z, core=core)
                    if move == "core":
                        to["core"] = 1 - core
                    elif move == "y2h":
                        to["y"] = y ^ 2
                    else:
                        to[move[0]] ^= (FIRST if move[1] == "1" else SECOND)[core]
                    pairs.append((device_at(x, y, z, core), device_at(**to)))
    return pairs


def swap(value, move):
    return lax.ppermute(value, ("aa", "col"), flipped(move))


def grown(value, move):
    return jnp.concatenate([value, swap(value, move)], axis=0)


def split(value):
    high = value.astype(BF16)
    return high, (value - high.astype(F32)).astype(BF16)


def dot(a, b):
    return jnp.dot(a, b, preferred_element_type=F32)


def dot3(a_high, a_low, b_high, b_low):
    return dot(a_high, b_high) + (dot(a_high, b_low) + dot(a_low, b_high))


def position():
    aa, col = lax.axis_index("aa"), lax.axis_index("col")
    y = (aa // 8) * 2 + col % 2
    return (aa // 2) % 4, y, col // 2, aa % 2


def chosen(core, pair):
    return jnp.where(core == 0, pair[0], pair[1])


def bit(j, at):
    return (j >> at) & 1


def amplitude_d(j, half, core, x, y):
    first, second = chosen(core, FIRST), chosen(core, SECOND)
    high = (y // 2) ^ bit(j, 0)
    x = x ^ (bit(j, 1) * first) ^ (half * second)
    return ((high * 4 + x) * 2 + core) * 2


def kernel(*refs, n_fit, n_amp, a_size, k_size, b_size):
    where_ref, a_ref = refs[0], refs[1]
    fits = refs[2 : 2 + n_fit]
    amps = refs[2 + n_fit : 2 + n_fit + n_amp]
    r_ref, fh, fl, f8, ah, a8, xh, xl, th, tl, vs, ts = refs[2 + n_fit + n_amp :]
    step = pl.program_id(0)
    last = pl.num_programs(0) - 1
    x, y, z, core = (where_ref[i] for i in range(4))
    c_size, (q_size, columns) = C_STEP, fh.shape
    pairs = th.shape[2]

    @pl.when(step == 0)
    def _():
        for other in range(2):
            owner = core if other == 0 else 1 - core
            first, second = chosen(owner, FIRST), chosen(owner, SECOND)

            def reached(at):
                froms = [at, at ^ second]
                lower = [jnp.minimum(v, v ^ first) for v in froms]
                return [lower, [v ^ first for v in lower]]

            at_x = [[v * 256 + owner * 128 for v in row] for row in reached(x)]
            at_y = [[(v // 2) * 1024 + (v % 2) * 16 for v in row] for row in reached(y)]
            at_z = [[v * 32 for v in row] for row in reached(z)]
            for at, ref in enumerate(fits):
                part, half = at // 4, (at // 2) % 2
                if at % 2 != other:
                    continue
                cols = slice(CUTS[part], CUTS[part + 1])
                for j in range(32):
                    flips = dict(zip(ORDERS[part], (bit(j, 3), bit(j, 4), half)))
                    rows = at_x[bit(j, 2)][flips["x"]] + at_y[bit(j, 1)][flips["y"]] + at_z[bit(j, 0)][flips["z"]]
                    place = pl.ds(pl.multiple_of(rows, 16), 16)
                    high, low = split(ref[j])
                    fh[place, cols] = high
                    fl[place, cols] = low

        def narrow(i, carry):
            rows = pl.ds(pl.multiple_of(i * 32, 32), 32)
            f8[rows, :] = (fl[rows, :].astype(F32) * F_LOW).astype(F8)
            f8[pl.ds(pl.multiple_of(q_size + i * 32, 32), 32), :] = (fh[rows, :].astype(F32) * F_HIGH).astype(F8)
            return carry

        lax.fori_loop(0, q_size // 32, narrow, 0, unroll=2)
        r_ref[...] = jnp.zeros_like(r_ref)

    lane = lax.broadcasted_iota(jnp.int32, (a_size, LANES), 1)
    front, even = lane < 64, (lane // 32) % 2 == 0

    def fit_ready():
        for i in range(0, a_size, 4):
            rows = slice(i * c_size, (i + 4) * c_size)
            value = a_ref[i : i + 4].reshape(4 * c_size, q_size)
            high = value.astype(BF16)
            ah[rows, :] = high
            a8[rows, :q_size] = (value * A_HIGH).astype(F8)
            a8[rows, q_size:] = ((value - high.astype(F32)) * A_LOW).astype(F8)

    def first_parts():
        values = [None] * (columns // N_STEP)

        def one(n):
            cols = slice(n * N_STEP, (n + 1) * N_STEP)
            values[n] = dot(ah[...], fh[:, cols])

        def rest(n):
            cols = slice(n * N_STEP, (n + 1) * N_STEP)
            values[n] = values[n] + dot(a8[...], f8[:, cols]) * UNSCALE

        return values, [functools.partial(f, n) for n in range(len(values)) for f in (one, rest)]

    def store(values):
        for n, value in enumerate(values):
            for lt in range(N_STEP // LANES):
                vs[n * (N_STEP // LANES) + lt] = value[:, lt * LANES : (lt + 1) * LANES]

    def amplitudes_ready(k):
        for at, ref in enumerate(amps):
            half, owner = at // 2, (core if at % 2 == 0 else 1 - core)
            for j in range(4):
                d = amplitude_d(jnp.int32(j), half, owner, x, y)
                for dl in range(2):
                    rows = pl.ds(pl.multiple_of((d + dl) * c_size, c_size), c_size)
                    for lt in range(ts.shape[1]):
                        ts[k, lt, rows, :] = ref[j, k, dl, :, lt * LANES : (lt + 1) * LANES]
        for c in range(c_size):
            for lt in range(ts.shape[1]):
                high, low = split(ts[k, lt, pl.ds(c, ND, stride=c_size), :])
                rows, lanes = slice(c * ND, (c + 1) * ND), slice(lt * LANES, (lt + 1) * LANES)
                th[k, rows, lanes] = high
                tl[k, rows, lanes] = low

    def turned(tile, cq):
        q = [vs[tile, pl.ds(cq * 4 + j, a_size, stride=c_size), :] for j in range(4)]
        s = [
            jnp.where(front, q[0], pltpu.roll(q[2], 64, 1)),
            jnp.where(front, q[1], pltpu.roll(q[3], 64, 1)),
            jnp.where(front, pltpu.roll(q[0], 64, 1), q[2]),
            jnp.where(front, pltpu.roll(q[1], 64, 1), q[3]),
        ]
        w = [
            jnp.where(even, s[0], pltpu.roll(s[1], 32, 1)),
            jnp.where(even, pltpu.roll(s[0], 96, 1), s[1]),
            jnp.where(even, s[2], pltpu.roll(s[3], 32, 1)),
            jnp.where(even, pltpu.roll(s[2], 96, 1), s[3]),
        ]
        for b in range(4):
            high, low = split(w[b])
            row = (tile * 4 + b) * a_size
            xh[row : row + a_size, cq * LANES : (cq + 1) * LANES] = high
            xl[row : row + a_size, cq * LANES : (cq + 1) * LANES] = low

    def second_parts():
        return [functools.partial(amplitudes_ready, k) for k in range(k_size)] + [
            functools.partial(turned, tile, cq)
            for tile in range(columns // LANES)
            for cq in range(c_size // 4)
        ]

    def second_product():
        for k in range(k_size):
            rows = slice(k * b_size * a_size, (k + 1) * b_size * a_size)
            value = dot3(xh[rows, :], xl[rows, :], th[k], tl[k])
            r_ref[:, k] += value.reshape(b_size, a_size, pairs)

    @pl.when(step == 0)
    def _():
        fit_ready()
        values, parts = first_parts()
        for part in parts:
            part()
        store(values)

    @pl.when((step > 0) & (step < last))
    def _():
        fit_ready()
        values, dots = first_parts()
        moves = second_parts()
        for at, part in enumerate(dots):
            part()
            for move in moves[at * len(moves) // len(dots) : (at + 1) * len(moves) // len(dots)]:
                move()
        second_product()
        store(values)

    @pl.when(step == last)
    def _():
        for move in second_parts():
            move()
        second_product()


def contracted(where, fit_ac, fits, amps):
    a_size, c_local, q_size = fit_ac.shape
    k_size, pairs = amps[0].shape[1], amps[0].shape[4]
    columns = CUTS[-1]
    b_size = columns // (k_size * ND)
    rows = a_size * C_STEP
    steps = c_local // C_STEP
    whole = lambda value: pl.BlockSpec(
        value.shape, lambda i, w: (0,) * value.ndim, pipeline_mode=pl.Buffered(1)
    )
    grid_spec = pltpu.PrefetchScalarGridSpec(
        num_scalar_prefetch=1,
        grid=(steps + 1,),
        in_specs=[pl.BlockSpec((a_size, C_STEP, q_size), lambda i, w: (0, jnp.minimum(i, steps - 1), 0))]
        + [whole(value) for value in fits]
        + [
            pl.BlockSpec(
                (4, k_size, 2, C_STEP, pairs), lambda i, w: (0, 0, 0, jnp.maximum(i - 1, 0), 0)
            )
            for _ in amps
        ],
        out_specs=pl.BlockSpec((b_size, k_size, a_size, pairs), lambda i, w: (0, 0, 0, 0)),
        scratch_shapes=[
            pltpu.VMEM((q_size, columns), BF16),
            pltpu.VMEM((q_size, columns), BF16),
            pltpu.VMEM((2 * q_size, columns), F8),
            pltpu.VMEM((rows, q_size), BF16),
            pltpu.VMEM((rows, 2 * q_size), F8),
            pltpu.VMEM((k_size * b_size * a_size, C_STEP * ND), BF16),
            pltpu.VMEM((k_size * b_size * a_size, C_STEP * ND), BF16),
            pltpu.VMEM((k_size, C_STEP * ND, pairs), BF16),
            pltpu.VMEM((k_size, C_STEP * ND, pairs), BF16),
            pltpu.VMEM((columns // LANES, rows, LANES), F32),
            pltpu.VMEM((k_size, pairs // LANES, ND * C_STEP, LANES), F32),
        ],
    )
    return pl.pallas_call(
        functools.partial(
            kernel, n_fit=len(fits), n_amp=len(amps), a_size=a_size, k_size=k_size, b_size=b_size
        ),
        grid_spec=grid_spec,
        out_shape=jax.ShapeDtypeStruct((b_size, k_size, a_size, pairs), F32),
        compiler_params=pltpu.CompilerParams(vmem_limit_bytes=58 << 20),
    )(where, fit_ac, *fits, *amps)


def sent_to_all(value, groups):
    copies = jnp.broadcast_to(value, (len(groups[0]), *value.shape))
    return lax.all_to_all(copies, ("aa", "col"), 0, 0, tiled=True, axis_index_groups=groups)


def cubes():
    pairs = [[(0, 1), (2, 3)], [(0, 3), (1, 2)]]
    return [
        [device_at(x, y, z, core) for x in xs for y in ys for z in zs]
        for core in range(2)
        for xs in pairs[core]
        for ys in pairs[core]
        for zs in pairs[core]
    ]


def gathered_fit(fit_bd):
    value = sent_to_all(fit_bd, cubes())
    value = grown(value, "x2")
    parts = [value[:, :, CUTS[i] : CUTS[i + 1]] for i in range(len(ORDERS))]
    parts = [grown(part, order[1] + "2") for part, order in zip(parts, ORDERS)]
    arrived = [swap(part, order[2] + "2") for part, order in zip(parts, ORDERS)]
    near = [swap(part, "core") for part in parts]
    far = [swap(part, "core") for part in arrived]
    return [v for four in zip(parts, near, arrived, far) for v in four]


def gathered_amplitudes(amplitudes):
    value = amplitudes[None]
    value = grown(value, "y2h")
    value = grown(value, "x1")
    arrived = swap(value, "x2")
    return [value, swap(value, "core"), arrived, swap(arrived, "core")]


def shards(fit_ac, fit_bd, amplitudes):
    x, y, z, core = position()
    where = jnp.stack([x, y, z, core]).astype(jnp.int32)
    fits = gathered_fit(fit_bd)
    amps = gathered_amplitudes(amplitudes)
    partial = contracted(where, fit_ac, fits, amps)
    b_size, k_size, a_size, pairs = partial.shape
    peers = lax.axis_size("col")
    pieces = partial.reshape(peers, b_size // peers, k_size, a_size, pairs)
    pieces = lax.all_to_all(pieces, "col", 0, 0, tiled=True)
    return jnp.sum(pieces, axis=0).transpose(1, 0, 2, 3)


def solution(mesh):
    placed = (P("aa", "col", None), P(("aa", "col"), None), P(None, "aa", "col", None))
    return jax.shard_map(
        shards, mesh=mesh, in_specs=placed, out_specs=P(None, "col", "aa", None), check_vma=False
    )
```

```python
import functools

import jax
import jax.numpy as jnp
from jax import lax
from jax.experimental import pallas as pl
from jax.experimental.pallas import tpu as pltpu
from jax.sharding import PartitionSpec as P

BF16 = jnp.bfloat16
F32 = jnp.float32
ND = 32
LANES = 128
C_STEP = 8
N_STEP = 256
F8 = jnp.float8_e5m2
F_HIGH, F_LOW = 2.0**12, 2.0**21
A_HIGH, A_LOW = 2.0**17, 2.0**26
UNSCALE = 2.0**-38
CUTS = (0, 512, 1024)
ORDERS = ("xyz", "xzy")
T_ORDER = ("y2", "x1", "x2")
FIRST = (1, 3)
SECOND = (3, 1)


def device_at(x, y, z, core):
    return (((y // 2) * 4 + x) * 2 + core) * 8 + z * 2 + y % 2


def flipped(move):
    pairs = []
    for y in range(4):
        for x in range(4):
            for z in range(4):
                for core in range(2):
                    to = dict(x=x, y=y, z=z, core=core)
                    if move == "core":
                        to["core"] = 1 - core
                    elif move == "y2h":
                        to["y"] = y ^ 2
                    else:
                        to[move[0]] ^= (FIRST if move[1] == "1" else SECOND)[core]
                    pairs.append((device_at(x, y, z, core), device_at(**to)))
    return pairs


def swap(value, move):
    return lax.ppermute(value, ("aa", "col"), flipped(move))


def grown(value, move):
    return jnp.concatenate([value, swap(value, move)], axis=0)


def split(value):
    high = value.astype(BF16)
    return high, (value - high.astype(F32)).astype(BF16)


def dot(a, b):
    return jnp.dot(a, b, preferred_element_type=F32)


def dot3(a_high, a_low, b_high, b_low):
    return dot(a_high, b_high) + (dot(a_high, b_low) + dot(a_low, b_high))


def position():
    aa, col = lax.axis_index("aa"), lax.axis_index("col")
    y = (aa // 8) * 2 + col % 2
    return (aa // 2) % 4, y, col // 2, aa % 2


def chosen(core, pair):
    return jnp.where(core == 0, pair[0], pair[1])


def bit(j, at):
    return (j >> at) & 1


def amplitude_d(j, half, core, x, y):
    first, second = chosen(core, FIRST), chosen(core, SECOND)
    high = (y // 2) ^ bit(j, 0)
    x = x ^ (bit(j, 1) * first) ^ (half * second)
    return ((high * 4 + x) * 2 + core) * 2


def kernel(*refs, n_fit, n_amp, a_size, k_size, b_size):
    where_ref, a_ref = refs[0], refs[1]
    fits = refs[2 : 2 + n_fit]
    amps = refs[2 + n_fit : 2 + n_fit + n_amp]
    r_ref, fh, fl, f8, ah, a8, xh, xl, th, tl, vs, ts = refs[2 + n_fit + n_amp :]
    step = pl.program_id(0)
    last = pl.num_programs(0) - 1
    x, y, z, core = (where_ref[i] for i in range(4))
    c_size, (q_size, columns) = C_STEP, fh.shape
    pairs = th.shape[2]

    @pl.when(step == 0)
    def _():
        for other in range(2):
            owner = core if other == 0 else 1 - core
            first, second = chosen(owner, FIRST), chosen(owner, SECOND)

            def reached(at):
                froms = [at, at ^ second]
                lower = [jnp.minimum(v, v ^ first) for v in froms]
                return [lower, [v ^ first for v in lower]]

            at_x = [[v * 256 + owner * 128 for v in row] for row in reached(x)]
            at_y = [[(v // 2) * 1024 + (v % 2) * 16 for v in row] for row in reached(y)]
            at_z = [[v * 32 for v in row] for row in reached(z)]
            for at, ref in enumerate(fits):
                part, half = at // 4, (at // 2) % 2
                if at % 2 != other:
                    continue
                cols = slice(CUTS[part], CUTS[part + 1])
                for j in range(32):
                    flips = dict(zip(ORDERS[part], (bit(j, 3), bit(j, 4), half)))
                    rows = at_x[bit(j, 2)][flips["x"]] + at_y[bit(j, 1)][flips["y"]] + at_z[bit(j, 0)][flips["z"]]
                    place = pl.ds(pl.multiple_of(rows, 16), 16)
                    high, low = split(ref[j])
                    fh[place, cols] = high
                    fl[place, cols] = low

        def narrow(i, carry):
            rows = pl.ds(pl.multiple_of(i * 32, 32), 32)
            f8[rows, :] = (fl[rows, :].astype(F32) * F_LOW).astype(F8)
            f8[pl.ds(pl.multiple_of(q_size + i * 32, 32), 32), :] = (fh[rows, :].astype(F32) * F_HIGH).astype(F8)
            return carry

        lax.fori_loop(0, q_size // 32, narrow, 0, unroll=2)
        r_ref[...] = jnp.zeros_like(r_ref)

    lane = lax.broadcasted_iota(jnp.int32, (a_size, LANES), 1)
    front, even = lane < 64, (lane // 32) % 2 == 0

    def fit_ready():
        for i in range(0, a_size, 4):
            rows = slice(i * c_size, (i + 4) * c_size)
            value = a_ref[i : i + 4].reshape(4 * c_size, q_size)
            high = value.astype(BF16)
            ah[rows, :] = high
            a8[rows, :q_size] = (value * A_HIGH).astype(F8)
            a8[rows, q_size:] = ((value - high.astype(F32)) * A_LOW).astype(F8)

    def first_parts():
        values = [None] * (columns // N_STEP)

        def one(n):
            cols = slice(n * N_STEP, (n + 1) * N_STEP)
            values[n] = dot(ah[...], fh[:, cols])

        def rest(n):
            cols = slice(n * N_STEP, (n + 1) * N_STEP)
            values[n] = values[n] + dot(a8[...], f8[:, cols]) * UNSCALE

        return values, [functools.partial(f, n) for n in range(len(values)) for f in (one, rest)]

    def store(values):
        for n, value in enumerate(values):
            for lt in range(N_STEP // LANES):
                vs[n * (N_STEP // LANES) + lt] = value[:, lt * LANES : (lt + 1) * LANES]

    def amplitudes_ready(k):
        for at, ref in enumerate(amps):
            half, owner = at // 2, (core if at % 2 == 0 else 1 - core)
            for j in range(4):
                d = amplitude_d(jnp.int32(j), half, owner, x, y)
                for dl in range(2):
                    rows = pl.ds(pl.multiple_of((d + dl) * c_size, c_size), c_size)
                    for lt in range(ts.shape[1]):
                        ts[k, lt, rows, :] = ref[j, k, dl, :, lt * LANES : (lt + 1) * LANES]
        for c in range(c_size):
            for lt in range(ts.shape[1]):
                high, low = split(ts[k, lt, pl.ds(c, ND, stride=c_size), :])
                rows, lanes = slice(c * ND, (c + 1) * ND), slice(lt * LANES, (lt + 1) * LANES)
                th[k, rows, lanes] = high
                tl[k, rows, lanes] = low

    def turned(tile, cq):
        q = [vs[tile, pl.ds(cq * 4 + j, a_size, stride=c_size), :] for j in range(4)]
        s = [
            jnp.where(front, q[0], pltpu.roll(q[2], 64, 1)),
            jnp.where(front, q[1], pltpu.roll(q[3], 64, 1)),
            jnp.where(front, pltpu.roll(q[0], 64, 1), q[2]),
            jnp.where(front, pltpu.roll(q[1], 64, 1), q[3]),
        ]
        w = [
            jnp.where(even, s[0], pltpu.roll(s[1], 32, 1)),
            jnp.where(even, pltpu.roll(s[0], 96, 1), s[1]),
            jnp.where(even, s[2], pltpu.roll(s[3], 32, 1)),
            jnp.where(even, pltpu.roll(s[2], 96, 1), s[3]),
        ]
        for b in range(4):
            high, low = split(w[b])
            row = (tile * 4 + b) * a_size
            xh[row : row + a_size, cq * LANES : (cq + 1) * LANES] = high
            xl[row : row + a_size, cq * LANES : (cq + 1) * LANES] = low

    def second_parts():
        return [functools.partial(amplitudes_ready, k) for k in range(k_size)] + [
            functools.partial(turned, tile, cq)
            for tile in range(columns // LANES)
            for cq in range(c_size // 4)
        ]

    def second_product():
        for k in range(k_size):
            rows = slice(k * b_size * a_size, (k + 1) * b_size * a_size)
            value = dot3(xh[rows, :], xl[rows, :], th[k], tl[k])
            r_ref[:, k] += value.reshape(b_size, a_size, pairs)

    @pl.when(step == 0)
    def _():
        fit_ready()
        values, parts = first_parts()
        for part in parts:
            part()
        store(values)

    @pl.when((step > 0) & (step < last))
    def _():
        fit_ready()
        values, dots = first_parts()
        moves = second_parts()
        for at, part in enumerate(dots):
            part()
            for move in moves[at * len(moves) // len(dots) : (at + 1) * len(moves) // len(dots)]:
                move()
        second_product()
        store(values)

    @pl.when(step == last)
    def _():
        for move in second_parts():
            move()
        second_product()


def contracted(where, fit_ac, fits, amps):
    a_size, c_local, q_size = fit_ac.shape
    k_size, pairs = amps[0].shape[1], amps[0].shape[4]
    columns = CUTS[-1]
    b_size = columns // (k_size * ND)
    rows = a_size * C_STEP
    steps = c_local // C_STEP
    whole = lambda value: pl.BlockSpec(
        value.shape, lambda i, w: (0,) * value.ndim, pipeline_mode=pl.Buffered(1)
    )
    grid_spec = pltpu.PrefetchScalarGridSpec(
        num_scalar_prefetch=1,
        grid=(steps + 1,),
        in_specs=[pl.BlockSpec((a_size, C_STEP, q_size), lambda i, w: (0, jnp.minimum(i, steps - 1), 0))]
        + [whole(value) for value in fits]
        + [
            pl.BlockSpec(
                (4, k_size, 2, C_STEP, pairs), lambda i, w: (0, 0, 0, jnp.maximum(i - 1, 0), 0)
            )
            for _ in amps
        ],
        out_specs=pl.BlockSpec((b_size, k_size, a_size, pairs), lambda i, w: (0, 0, 0, 0)),
        scratch_shapes=[
            pltpu.VMEM((q_size, columns), BF16),
            pltpu.VMEM((q_size, columns), BF16),
            pltpu.VMEM((2 * q_size, columns), F8),
            pltpu.VMEM((rows, q_size), BF16),
            pltpu.VMEM((rows, 2 * q_size), F8),
            pltpu.VMEM((k_size * b_size * a_size, C_STEP * ND), BF16),
            pltpu.VMEM((k_size * b_size * a_size, C_STEP * ND), BF16),
            pltpu.VMEM((k_size, C_STEP * ND, pairs), BF16),
            pltpu.VMEM((k_size, C_STEP * ND, pairs), BF16),
            pltpu.VMEM((columns // LANES, rows, LANES), F32),
            pltpu.VMEM((k_size, pairs // LANES, ND * C_STEP, LANES), F32),
        ],
    )
    return pl.pallas_call(
        functools.partial(
            kernel, n_fit=len(fits), n_amp=len(amps), a_size=a_size, k_size=k_size, b_size=b_size
        ),
        grid_spec=grid_spec,
        out_shape=jax.ShapeDtypeStruct((b_size, k_size, a_size, pairs), F32),
        compiler_params=pltpu.CompilerParams(vmem_limit_bytes=58 << 20),
    )(where, fit_ac, *fits, *amps)


def sent_to_all(value, groups):
    copies = jnp.broadcast_to(value, (len(groups[0]), *value.shape))
    return lax.all_to_all(copies, ("aa", "col"), 0, 0, tiled=True, axis_index_groups=groups)


def cubes():
    pairs = [[(0, 1), (2, 3)], [(0, 3), (1, 2)]]
    return [
        [device_at(x, y, z, core) for x in xs for y in ys for z in zs]
        for core in range(2)
        for xs in pairs[core]
        for ys in pairs[core]
        for zs in pairs[core]
    ]


def gathered_fit(value):
    value = grown(value, "x2")
    parts = [value[:, :, CUTS[i] : CUTS[i + 1]] for i in range(len(ORDERS))]
    parts = [grown(part, order[1] + "2") for part, order in zip(parts, ORDERS)]
    arrived = [swap(part, order[2] + "2") for part, order in zip(parts, ORDERS)]
    near = [swap(part, "core") for part in parts]
    far = [swap(part, "core") for part in arrived]
    return [v for four in zip(parts, near, arrived, far) for v in four]


def gathered_amplitudes(amplitudes):
    value = grown(amplitudes, "x1")
    arrived = swap(value, "x2")
    return [value, swap(value, "core"), arrived, swap(arrived, "core")]


def shards(fit_ac, fit_bd, amplitudes):
    x, y, z, core = position()
    where = jnp.stack([x, y, z, core]).astype(jnp.int32)
    near, doubled = lax.optimization_barrier(
        (sent_to_all(fit_bd, cubes()), grown(amplitudes[None], "y2h"))
    )
    fits = gathered_fit(near)
    amps = gathered_amplitudes(doubled)
    partial = contracted(where, fit_ac, fits, amps)
    b_size, k_size, a_size, pairs = partial.shape
    peers = lax.axis_size("col")
    pieces = partial.reshape(peers, b_size // peers, k_size, a_size, pairs)
    pieces = lax.all_to_all(pieces, "col", 0, 0, tiled=True)
    return jnp.sum(pieces, axis=0).transpose(1, 0, 2, 3)


def solution(mesh):
    placed = (P("aa", "col", None), P(("aa", "col"), None), P(None, "aa", "col", None))
    return jax.shard_map(
        shards, mesh=mesh, in_specs=placed, out_specs=P(None, "col", "aa", None), check_vma=False
    )
```
